32 devices in a mesh: row: 4 (over y, x), col: 8 (over z, core).
Axes of the slice: x: 2, y: 2, z: 4, core: 2. Of those that a mesh axis runs over, the one named last changes fastest.
Arguments:
- noise: float32 [2048, 3072], P('row', 'col'), may hold values from -30 to 30
- images: float32 [6144, 3072], P('col', 'row'), may hold values from -6 to 6
- time_index: int32 [2048], P('row'), may hold values from 0 to 999
- w_in: float32 [3072, 3072], P(None, 'col'), may hold values from -0.109375 to 0.109375
- time_gain: float32 [3072], P('col'), may hold values from -5 to 5
- w_out: float32 [3072, 3072], P('col'), may hold values from -0.109375 to 0.109375
Outputs:
- targets: float32 [2048, 3072], P('row', 'col')
- row_pot: float32 [2048], P('row')
- col_pot: float32 [6144], P('col')
- grad_in: float32 [3072, 3072], P('row', 'col')
- grad_time: float32 [3072], P('col')
- grad_out: float32 [3072, 3072], P('col', 'row')
- mse: float32 [], replicated
The draws below stay inside these ranges and needn't reach their ends.
All inputs are finite; a program needn't handle non-finite values.
Results may differ from the reference program's by a relative error of at most 0.0003.
Values sent between devices are 32-bit elements; how exact they have to be, the bound alone decides.
A program may use at most 128 MiB of HBM per device.

```python
import jax
import jax.numpy as jnp
from jax import lax

DIM = 3072
HID = 3072
ITERS = 2
TIMES = 1000
NOISE = 2048
IMAGES = 6144


def draw_noise(key, part):
    base = jax.random.normal(key, (NOISE, DIM), jnp.float32)
    return base


def place_ends(result, own_key, least, high):
    shape = result.shape
    spot = [jax.random.randint(jax.random.fold_in(own_key, axis), (), 0, shape[axis]) for axis in range(len(shape))]
    result = result.at[tuple(spot)].set(least)
    longest = shape.index(max(shape))
    spot[longest] = (spot[longest] + 1) % shape[longest]
    return result.at[tuple(spot)].set(high)


def block_scale(rng, extent, shards, low, top_value):
    factor_of, own = 1.0, jax.random.fold_in(rng, 6)
    for dim, blocks in shards:
        heights = jnp.exp(jax.random.uniform(jax.random.fold_in(own, dim), (blocks,), jnp.float32, low / len(shards), top_value / len(shards)))
        factor_of = factor_of * jnp.repeat(heights, extent[dim] // blocks).reshape([-1 if axis == dim else 1 for axis in range(len(extent))])
    return factor_of


def bell_draw(key, dims, width, bound, split=(), dtype=jnp.bfloat16):
    gain = block_scale(key, dims, split, -0.22, 0.18) if split else 1.0
    drawn = jax.random.normal(key, dims, jnp.float32) * width * gain
    return jnp.minimum(jnp.maximum(drawn, -bound), bound).astype(dtype)


def setup_inputs(seed: int = 0) -> dict:
    key_of = jax.random.split(jax.random.key(seed), 7)
    noise = draw_noise(jax.random.fold_in(key_of[6], 71), 0)
    images = bell_draw(key_of[1], (IMAGES, DIM), 1.0, 6.0, ((0, 8), (1, 4)), jnp.float32)
    time_index = place_ends(jax.random.randint(key_of[2], (NOISE,), 0, TIMES), jax.random.fold_in(key_of[2], 1), 0, TIMES - 1).astype(jnp.int32)
    w_in = bell_draw(key_of[3], (DIM, HID), DIM ** -0.5, 0.109375, ((1, 8),), jnp.float32)
    time_gain = bell_draw(key_of[4], (HID,), 1.0, 5.0, ((0, 8),), jnp.float32)
    w_out = bell_draw(key_of[5], (HID, DIM), HID ** -0.5, 0.109375, ((0, 8),), jnp.float32)
    return dict(noise=noise, images=images, time_index=time_index, w_in=w_in, time_gain=time_gain, w_out=w_out)


EPSILON = 0.01

def log_sum_exp(values, axis):
    peak = lax.optimization_barrier(jnp.max(values, axis=axis, keepdims=True))
    total = lax.optimization_barrier(jnp.sum(jnp.exp(values - peak), axis=axis, keepdims=True))
    return jnp.squeeze(jnp.log(total) + peak, axis=axis)

def reference(noise, images, time_index, w_in, time_gain, w_out):
    highest = lax.Precision.HIGHEST
    noise_norms = lax.optimization_barrier(jnp.sum(noise * noise, axis=1))
    image_norms = lax.optimization_barrier(jnp.sum(images * images, axis=1))
    cross = jnp.dot(noise, images.T, precision=highest, preferred_element_type=jnp.float32)
    scaled = (noise_norms[:, None] + image_norms[None, :] - 2.0 * cross) / (DIM * EPSILON)
    col_pot = jnp.zeros((IMAGES,), jnp.float32)
    row_pot = jnp.zeros((NOISE,), jnp.float32)
    for iteration in range(ITERS):
        row_pot = jnp.log(jnp.float32(IMAGES)) - log_sum_exp(col_pot[None, :] - scaled, 1)
        col_pot = jnp.log(jnp.float32(NOISE)) - log_sum_exp(row_pot[:, None] - scaled, 0)
    logits = col_pot[None, :] - scaled
    weights = jnp.exp(logits - log_sum_exp(logits, 1)[:, None])
    targets = jnp.dot(weights, images, precision=highest, preferred_element_type=jnp.float32)
    fraction = (time_index.astype(jnp.float32) + 0.5) / TIMES
    mixed = (1.0 - fraction)[:, None] * noise + fraction[:, None] * targets
    velocity = targets - noise
    pre = jnp.dot(mixed, w_in, precision=highest, preferred_element_type=jnp.float32) + fraction[:, None] * time_gain[None, :]
    sigma = jax.nn.sigmoid(pre)
    hidden = pre * sigma
    out = jnp.dot(hidden, w_out, precision=highest, preferred_element_type=jnp.float32)
    diff = out - velocity
    mse = jnp.sum(diff * diff) / (NOISE * DIM)
    slope = diff / jnp.sqrt(jnp.float32(NOISE))
    grad_out = jnp.dot(hidden.T, slope, precision=highest, preferred_element_type=jnp.float32)
    back = jnp.dot(slope, w_out.T, precision=highest, preferred_element_type=jnp.float32)
    dpre = back * sigma * (1.0 + pre * (1.0 - sigma))
    grad_in = jnp.dot(mixed.T, dpre, precision=highest, preferred_element_type=jnp.float32)
    grad_time = lax.optimization_barrier(jnp.sum(fraction[:, None] * dpre, axis=0))
    return (targets, row_pot, col_pot, grad_in, grad_time, grad_out, mse)
```

```python
import functools

import jax
import jax.numpy as jnp
from jax import lax
from jax.experimental import pallas as pl
from jax.experimental.pallas import tpu as pltpu
from jax.sharding import PartitionSpec as P

ITERS = 2
TIMES = 1000


EPSILON = 0.01
MESH = pl.DeviceIdType.MESH
VMEM_LIMIT = 60 * 1024 * 1024


def params(collective_id):
    return pltpu.CompilerParams(
        collective_id=collective_id, has_side_effects=True, vmem_limit_bytes=VMEM_LIMIT
    )


def remote(src, dst, send_sem, recv_sem, device):
    return pltpu.make_async_remote_copy(
        src_ref=src,
        dst_ref=dst,
        send_sem=send_sem,
        recv_sem=recv_sem,
        device_id=device,
        device_id_type=MESH,
    )


def flip(index):
    return index + 1 - 2 * lax.rem(index, 2)


def greet(devices):
    barrier = pltpu.get_barrier_semaphore()
    for device, condition in devices:
        def signal(device=device):
            pl.semaphore_signal(barrier, inc=1, device_id=device, device_id_type=MESH)
        if condition is None:
            signal()
        else:
            pl.when(condition)(signal)
    count = jnp.int32(0)
    for device, condition in devices:
        count = count + (1 if condition is None else jnp.where(condition, 1, 0))
    pl.semaphore_wait(barrier, count)


def gather_kernel(
    rows, chips, noise, images, all_noise, all_images,
    own_sem, right_send, right_recv, left_send, left_recv, pair_send, pair_recv, row_send, row_recv,
):
    r = lax.axis_index("row")
    c = lax.axis_index("col")
    z = c // 2
    core = lax.rem(c, 2)
    width = noise.shape[1]
    height, depth = images.shape
    half = height // 2

    def at(row, col):
        return {"row": row, "col": col}

    partner = at(r, flip(c))
    up = at(r, lax.rem(c + 2, 2 * chips))
    down = at(r, lax.rem(c + 2 * chips - 2, 2 * chips))
    others = [lax.rem(r + k, rows) for k in range(1, rows)]
    greet(
        [(partner, None), (up, z < chips - 1), (down, z > 0)]
        + [(at(other, c), None) for other in others]
    )

    def noise_slot(chip, parity):
        if len(all_noise.shape) == 3:
            return all_noise.at[chip * 2 + parity]
        start = pl.multiple_of((chip * 2 + parity) * width, width)
        return all_noise.at[:, pl.ds(start, width)]

    def image_slot(owner, first, count):
        start = pl.multiple_of(owner * depth, depth)
        return all_images.at[pl.ds(first, count), pl.ds(start, depth)]

    def go_up(src, s):
        chip = z - s
        return remote(src, noise_slot(chip, core), right_send.at[s], right_recv.at[s], up)

    def go_down(src, s):
        chip = z + s
        return remote(src, noise_slot(chip, core), left_send.at[s], left_recv.at[s], down)

    def go_pair(src, chip):
        return remote(src, noise_slot(chip, core), pair_send.at[chip], pair_recv.at[chip], partner)

    own_noise = pltpu.make_async_copy(noise, noise_slot(z, core), own_sem.at[0])
    own_images = pltpu.make_async_copy(images, image_slot(r, 0, height), own_sem.at[1])

    pl.when(z < chips - 1)(lambda: go_up(noise, 0).start())
    pl.when(z > 0)(lambda: go_down(noise, 0).start())

    if rows == 4:
        xn = flip(r)
        yn = lax.rem(r + 2, 4)
        dg = flip(yn)
        to_x, to_y = at(xn, c), at(yn, c)

        def part(src_ref, owner, second, k, target):
            first = half if second else 0
            src = images.at[pl.ds(first, half), :] if src_ref is None else image_slot(owner, first, half)
            return remote(
                src, image_slot(owner, first, half), row_send.at[k], row_recv.at[k], target
            )

        first_x, first_y = part(None, r, False, 0, to_x), part(None, r, True, 1, to_y)
        second_x, second_y = part(None, r, True, 2, to_x), part(None, r, False, 3, to_y)
        first_x.start()
        first_y.start()
        second_x.start()
        second_y.start()
        pass_y, pass_x = part(0, xn, False, 4, to_y), part(0, yn, True, 5, to_x)
        in_first_x, in_first_y = part(None, xn, False, 0, to_x), part(None, yn, True, 1, to_y)
        in_second_x, in_second_y = part(None, xn, True, 2, to_x), part(None, yn, False, 3, to_y)
        in_pass_y, in_pass_x = part(None, dg, False, 4, to_y), part(None, dg, True, 5, to_x)
    else:
        sends = [
            remote(images, image_slot(r, 0, height), row_send.at[k], row_recv.at[k], at(other, c))
            for k, other in enumerate(others)
        ]
        for copy in sends:
            copy.start()

    own_noise.start()
    own_images.start()
    go_pair(noise, z).start()

    for s in range(chips - 1):
        from_down = z - 1 - s >= 0
        from_up = z + 1 + s < chips

        def arrived_up(s=s):
            chip = z - 1 - s
            remote(noise, noise_slot(chip, core), right_send.at[s], right_recv.at[s], up).wait_recv()
            if s + 1 < chips - 1:
                pl.when(z < chips - 1)(lambda: go_up(noise_slot(chip, core), s + 1).start())
            go_pair(noise_slot(chip, core), chip).start()

        def arrived_down(s=s):
            chip = z + 1 + s
            remote(noise, noise_slot(chip, core), left_send.at[s], left_recv.at[s], down).wait_recv()
            if s + 1 < chips - 1:
                pl.when(z > 0)(lambda: go_down(noise_slot(chip, core), s + 1).start())
            go_pair(noise_slot(chip, core), chip).start()

        pl.when(from_down)(arrived_up)
        pl.when(from_up)(arrived_down)
        if rows == 4 and s == min(1, chips - 2):
            in_first_x.wait_recv()
            pass_y.start()
            in_first_y.wait_recv()
            pass_x.start()

    if rows == 4:
        for copy in (in_second_x, in_second_y, in_pass_y, in_pass_x):
            copy.wait_recv()
        for copy in (first_x, first_y, second_x, second_y, pass_y, pass_x):
            copy.wait_send()
    else:
        for k, other in enumerate(others):
            source = lax.rem(r + rows - 1 - k, rows)
            remote(
                images, image_slot(source, 0, height), row_send.at[k], row_recv.at[k], at(other, c)
            ).wait_recv()
        for copy in sends:
            copy.wait_send()

    own_noise.wait()
    own_images.wait()
    for s in range(chips - 1):
        pl.when(jnp.logical_and(z < chips - 1, z - s >= 0))(lambda s=s: go_up(noise, s).wait_send())
        pl.when(jnp.logical_and(z > 0, z + s < chips))(lambda s=s: go_down(noise, s).wait_send())
    for chip in range(chips):
        copy = remote(
            noise, noise_slot(chip, 1 - core), pair_send.at[chip], pair_recv.at[chip], partner
        )
        copy.wait_send()
        copy.wait_recv()


def gathered(noise, images, rows, cols):
    chips = cols // 2
    dma = pltpu.SemaphoreType.DMA
    anywhere = pl.BlockSpec(memory_space=pl.ANY)
    inside = pl.BlockSpec(memory_space=pltpu.VMEM)
    steps = max(chips - 1, 1)
    points, width = noise.shape
    stacked = width % 128 != 0
    full_noise, full_images = pl.pallas_call(
        functools.partial(gather_kernel, rows, chips),
        out_shape=(
            jax.ShapeDtypeStruct(
                (cols, points, width) if stacked else (points, width * cols), jnp.float32
            ),
            jax.ShapeDtypeStruct((images.shape[0], images.shape[1] * rows), jnp.float32),
        ),
        in_specs=[inside, inside],
        out_specs=(anywhere, anywhere),
        scratch_shapes=[
            dma((2,)), dma((steps,)), dma((steps,)), dma((steps,)), dma((steps,)),
            dma((chips,)), dma((chips,)), dma((max(rows, 6),)), dma((max(rows, 6),)),
        ],
        compiler_params=params(0),
        name="gather",
    )(noise, images)
    if stacked:
        full_noise = jnp.swapaxes(full_noise, 0, 1).reshape(points, width * cols)
    return full_noise, full_images


def sinkhorn_kernel(
    rows, cols, noise_count, image_count, scaled, weights, row_out, col_out,
    row_mine, row_all, col_mine, col_all, stat_peak, stat_total, pots,
    row_send, row_recv, col_send, col_recv,
):
    r = lax.axis_index("row")
    c = lax.axis_index("col")
    points, pictures = scaled.shape
    slab = 64
    slabs = points // slab

    def at(row, col):
        return {"row": row, "col": col}

    row_peers = [at(r, lax.rem(c + k, cols)) for k in range(1, cols)]
    col_peers = [at(lax.rem(r + k, rows), c) for k in range(1, rows)]
    greet([(peer, None) for peer in row_peers + col_peers])

    def exchange(mine, everything, send, recv, peers, position, turn):
        count = len(peers) + 1
        copies = [
            remote(mine.at[turn], everything.at[turn, position], send.at[turn, k], recv.at[turn, k], peer)
            for k, peer in enumerate(peers)
        ]
        for copy in copies:
            copy.start()
        for k, peer in enumerate(peers):
            source = lax.rem(position + count - 1 - k, count)
            remote(
                mine.at[turn], everything.at[turn, source], send.at[turn, k], recv.at[turn, k], peer
            ).wait_recv()
        for copy in copies:
            copy.wait_send()
        peak, total = mine[turn, 0:1, :], mine[turn, 1:2, :]
        sources = [lax.rem(position + k, count) for k in range(1, count)]
        pairs = [everything[turn, source] for source in sources]
        top = peak
        for pair in pairs:
            top = jnp.maximum(top, pair[0:1])
        whole = total * jnp.exp(peak - top)
        for pair in pairs:
            whole = whole + pair[1:2] * jnp.exp(pair[0:1] - top)
        return jnp.log(whole) + top

    def over_images(col_pot, turn):
        def step(i, carry):
            window = pl.ds(pl.multiple_of(i * slab, slab), slab)
            logits = col_pot - scaled[window, :]
            peak = jnp.max(logits, axis=1, keepdims=True)
            total = jnp.sum(jnp.exp(logits - peak), axis=1, keepdims=True)
            stat_peak[window, :] = jnp.broadcast_to(peak, (slab, 128))
            stat_total[window, :] = jnp.broadcast_to(total, (slab, 128))
            return carry

        lax.fori_loop(0, slabs, step, 0)
        row_mine[turn, 0:1, :] = stat_peak[...].T[0:1, :]
        row_mine[turn, 1:2, :] = stat_total[...].T[0:1, :]
        return exchange(row_mine, row_all, row_send, row_recv, row_peers, c, turn)

    def as_column(line):
        pots[...] = jnp.broadcast_to(line, (128, points)).T

    def over_noise(turn):
        def top_of(i, peak):
            window = pl.ds(pl.multiple_of(i * slab, slab), slab)
            logits = pots[window, 0:1] - scaled[window, :]
            return jnp.maximum(peak, jnp.max(logits, axis=0, keepdims=True))

        peak = lax.fori_loop(0, slabs, top_of, jnp.full((1, pictures), -jnp.inf, jnp.float32))

        def sum_of(i, total):
            window = pl.ds(pl.multiple_of(i * slab, slab), slab)
            logits = pots[window, 0:1] - scaled[window, :]
            return total + jnp.sum(jnp.exp(logits - peak), axis=0, keepdims=True)

        total = lax.fori_loop(0, slabs, sum_of, jnp.zeros((1, pictures), jnp.float32))
        col_mine[turn, 0:1, :] = peak
        col_mine[turn, 1:2, :] = total
        return exchange(col_mine, col_all, col_send, col_recv, col_peers, r, turn)

    col_pot = jnp.zeros((1, pictures), jnp.float32)
    for turn in range(ITERS):
        row_pot = jnp.log(jnp.float32(image_count)) - over_images(col_pot, turn)
        as_column(row_pot)
        col_pot = jnp.log(jnp.float32(noise_count)) - over_noise(turn)
    row_out[...] = row_pot
    col_out[...] = col_pot
    as_column(over_images(col_pot, ITERS))

    def weigh(i, carry):
        window = pl.ds(pl.multiple_of(i * slab, slab), slab)
        weights[window, :] = jnp.exp(col_pot - scaled[window, :] - pots[window, 0:1])
        return carry

    lax.fori_loop(0, slabs, weigh, 0)


def coupled(scaled, rows, cols):
    points, pictures = scaled.shape
    dma = pltpu.SemaphoreType.DMA
    inside = pl.BlockSpec(memory_space=pltpu.VMEM)
    turns = ITERS + 1
    weights, row_pot, col_pot = pl.pallas_call(
        functools.partial(sinkhorn_kernel, rows, cols, points * rows, pictures * cols),
        out_shape=(
            jax.ShapeDtypeStruct((points, pictures), jnp.float32),
            jax.ShapeDtypeStruct((1, points), jnp.float32),
            jax.ShapeDtypeStruct((1, pictures), jnp.float32),
        ),
        in_specs=[inside],
        out_specs=(inside, inside, inside),
        scratch_shapes=[
            pltpu.VMEM((turns, 2, points), jnp.float32),
            pltpu.VMEM((turns, cols, 2, points), jnp.float32),
            pltpu.VMEM((ITERS, 2, pictures), jnp.float32),
            pltpu.VMEM((ITERS, rows, 2, pictures), jnp.float32),
            pltpu.VMEM((points, 128), jnp.float32),
            pltpu.VMEM((points, 128), jnp.float32),
            pltpu.VMEM((points, 128), jnp.float32),
            dma((turns, cols)), dma((turns, cols)), dma((ITERS, rows)), dma((ITERS, rows)),
        ],
        compiler_params=params(1),
        name="sinkhorn",
    )(scaled)
    return weights, row_pot[0], col_pot[0]


def total_kernel(
    chips, count, part, whole, own, other, going, coming,
    load_sem, keep_sem, pair_send, pair_recv, sum_send, sum_recv,
    cast_send, cast_recv, share_send, share_recv,
):
    r = lax.axis_index("row")
    c = lax.axis_index("col")
    z = c // 2
    core = lax.rem(c, 2)
    points, features = part.shape
    width = features // 2
    tall = points // count
    per_way = count // 2
    last = chips - 1

    def at(col):
        return {"row": r, "col": col}

    partner = at(flip(c))
    up = at(lax.rem(c + 2, 2 * chips))
    down = at(lax.rem(c + 2 * chips - 2, 2 * chips))
    greet([(partner, None), (up, z < last), (down, z > 0)])

    mine = pl.multiple_of(core * width, width)
    theirs = pl.multiple_of((1 - core) * width, width)

    def rows_of(j):
        return pl.ds(pl.multiple_of(j * tall, tall), tall)

    def load(j):
        return pltpu.make_async_copy(
            part.at[rows_of(j), pl.ds(mine, width)], own.at[rows_of(j), :], load_sem.at[j]
        )

    def pair(j):
        return remote(
            part.at[rows_of(j), pl.ds(theirs, width)], other.at[rows_of(j), :],
            pair_send.at[j], pair_recv.at[j], partner,
        )

    def start(j, carry):
        pair(j).start()
        load(j).start()
        return carry

    lax.fori_loop(0, count, start, 0)

    def reduce_step(j, first, final, onward):
        load(j).wait()
        pair(j).wait_recv()
        window = rows_of(j)

        @pl.when(first)
        def _():
            going[window, :] = own[window, :] + other[window, :]

        @pl.when(jnp.logical_not(first))
        def _():
            hop(j, onward).wait_recv()
            going[window, :] = own[window, :] + other[window, :] + coming[window, :]

        @pl.when(jnp.logical_not(final))
        def _():
            hop(j, onward).start()

    def hop(j, target):
        return remote(
            going.at[rows_of(j), :], coming.at[rows_of(j), :], sum_send.at[j], sum_recv.at[j], target
        )

    def spot(j, start_col):
        return whole.at[rows_of(j), pl.ds(start_col, width)]

    def cast(j, target):
        return remote(spot(j, mine), spot(j, mine), cast_send.at[j], cast_recv.at[j], target)

    def cast_first(j, target):
        return remote(going.at[rows_of(j), :], spot(j, mine), cast_send.at[j], cast_recv.at[j], target)

    def share(j):
        return remote(spot(j, mine), spot(j, mine), share_send.at[j], share_recv.at[j], partner)

    def share_first(j):
        return remote(going.at[rows_of(j), :], spot(j, mine), share_send.at[j], share_recv.at[j], partner)

    def keep(j):
        return pltpu.make_async_copy(going.at[rows_of(j), :], spot(j, mine), keep_sem.at[j])

    def way(step, here, parity, onward, back):
        j = step - here

        @pl.when(jnp.logical_and(j >= 0, j < per_way))
        def _():
            index = 2 * j + parity
            reduce_step(index, here == 0, here == last, onward)

            @pl.when(here == last)
            def _():
                cast_first(index, back).start()
                keep(index).start()
                share_first(index).start()

        k = step - (2 * last - here)

        @pl.when(jnp.logical_and(jnp.logical_and(k >= 0, k < per_way), here < last))
        def _():
            index = 2 * k + parity
            cast(index, back).wait_recv()

            @pl.when(here > 0)
            def _():
                cast(index, back).start()

            share(index).start()

    def step(s, carry):
        way(s, z, 0, up, down)
        way(s, last - z, 1, down, up)
        return carry

    lax.fori_loop(0, per_way + 2 * last, step, 0)

    def finish(j, carry):
        pair(j).wait_send()
        share(j).wait_send()
        remote(
            spot(j, mine), spot(j, theirs), share_send.at[j], share_recv.at[j], partner
        ).wait_recv()
        here = jnp.where(lax.rem(j, 2) == 0, z, last - z)

        @pl.when(here < last)
        def _():
            hop(j, partner).wait_send()

        @pl.when(here == last)
        def _():
            keep(j).wait()

        @pl.when(here > 0)
        def _():
            cast(j, partner).wait_send()

        return carry

    lax.fori_loop(0, count, finish, 0)


def total_over_col(part, cols, collective_id):
    points, features = part.shape
    chips = cols // 2
    count = points // 16
    dma = pltpu.SemaphoreType.DMA
    anywhere = pl.BlockSpec(memory_space=pl.ANY)
    return pl.pallas_call(
        functools.partial(total_kernel, chips, count),
        out_shape=jax.ShapeDtypeStruct((points, features), jnp.float32),
        in_specs=[anywhere],
        out_specs=anywhere,
        scratch_shapes=[pltpu.VMEM((points, features // 2), jnp.float32)] * 4 + [dma((count,))] * 10,
        compiler_params=params(collective_id),
        name=f"total{collective_id}",
    )(part)


def body(rows, cols, noise, images, time_index, w_in, time_gain, w_out):
    high = lax.Precision.HIGH
    full_noise, full_images = gathered(noise, images, rows, cols)
    width = full_noise.shape[1]
    noise_count = full_noise.shape[0] * rows
    noise_norms = jnp.sum(full_noise * full_noise, axis=1)
    image_norms = jnp.sum(full_images * full_images, axis=1)
    cross = lax.dot_general(
        full_noise,
        full_images,
        (((1,), (1,)), ((), ())),
        precision=high,
        preferred_element_type=jnp.float32,
    )
    scaled = (noise_norms[:, None] + image_norms[None, :] - 2.0 * cross) / (width * EPSILON)
    weights, row_pot, col_pot = coupled(scaled, rows, cols)
    partial_value = jnp.dot(
        weights, full_images, precision=high, preferred_element_type=jnp.float32
    )
    slice_width = noise.shape[1]
    slice_start = lax.axis_index("col") * slice_width
    whole_targets = total_over_col(partial_value, cols, 2)
    targets = lax.dynamic_slice_in_dim(whole_targets, slice_start, slice_width, 1)
    fraction = (time_index.astype(jnp.float32) + 0.5) / TIMES
    mixed = (1.0 - fraction)[:, None] * full_noise + fraction[:, None] * whole_targets
    velocity = whole_targets - full_noise
    pre = (
        jnp.dot(mixed, w_in, precision=high, preferred_element_type=jnp.float32)
        + fraction[:, None] * time_gain[None, :]
    )
    sigma = jax.nn.sigmoid(pre)
    hidden = pre * sigma
    part_out = jnp.dot(hidden, w_out, precision=high, preferred_element_type=jnp.float32)
    out = total_over_col(part_out, cols, 3)
    diff = out - velocity
    squared = jnp.sum(diff * diff)
    slope = diff / jnp.sqrt(jnp.float32(noise_count))
    local_out = lax.dot_general(
        hidden,
        slope,
        (((0,), (0,)), ((), ())),
        precision=high,
        preferred_element_type=jnp.float32,
    )
    back = lax.dot_general(
        slope,
        w_out,
        (((1,), (1,)), ((), ())),
        precision=high,
        preferred_element_type=jnp.float32,
    )
    dpre = back * sigma * (1.0 + pre * (1.0 - sigma))
    local_in = lax.dot_general(
        mixed, dpre, (((0,), (0,)), ((), ())), precision=high, preferred_element_type=jnp.float32
    )
    local_time = jnp.sum(fraction[:, None] * dpre, axis=0)
    grad_in, grad_out = (
        lax.psum_scatter(local_in, "row", scatter_dimension=0, tiled=True),
        lax.psum_scatter(local_out, "row", scatter_dimension=1, tiled=True),
    )
    grad_time, squared_all = lax.psum((local_time, squared), "row")
    mse = squared_all / (noise_count * width)
    return (targets, row_pot, col_pot, grad_in, grad_time, grad_out, mse)


def solution(mesh):
    placed = (P("row", "col"), P("col", "row"), P("row"), P(None, "col"), P("col"), P("col", None))
    return jax.shard_map(
        functools.partial(body, mesh.shape["row"], mesh.shape["col"]),
        mesh=mesh,
        in_specs=placed,
        out_specs=(
            P("row", "col"),
            P("row"),
            P("col"),
            P("row", "col"),
            P("col"),
            P("col", "row"),
            P(),
        ),
        check_vma=False,
    )
```

```python
import functools

import jax
import jax.numpy as jnp
from jax import lax
from jax.experimental import pallas as pl
from jax.experimental.pallas import tpu as pltpu
from jax.sharding import PartitionSpec as P

ITERS = 2
TIMES = 1000


EPSILON = 0.01
TALL = 16
SLACK = 2
MESH = pl.DeviceIdType.MESH
VMEM_LIMIT = 60 * 1024 * 1024


def params(collective_id):
    return pltpu.CompilerParams(
        collective_id=collective_id, has_side_effects=True, vmem_limit_bytes=VMEM_LIMIT
    )


def remote(src, dst, send_sem, recv_sem, device):
    return pltpu.make_async_remote_copy(
        src_ref=src,
        dst_ref=dst,
        send_sem=send_sem,
        recv_sem=recv_sem,
        device_id=device,
        device_id_type=MESH,
    )


def flip(index):
    return index + 1 - 2 * lax.rem(index, 2)


def greet(devices):
    barrier = pltpu.get_barrier_semaphore()
    for device, condition in devices:
        def signal(device=device):
            pl.semaphore_signal(barrier, inc=1, device_id=device, device_id_type=MESH)
        if condition is None:
            signal()
        else:
            pl.when(condition)(signal)
    count = jnp.int32(0)
    for device, condition in devices:
        count = count + (1 if condition is None else jnp.where(condition, 1, 0))
    pl.semaphore_wait(barrier, count)


def gather_kernel(
    rows, chips, noise, images, all_noise, all_images,
    own_sem, right_send, right_recv, left_send, left_recv, pair_send, pair_recv, row_send, row_recv,
):
    r = lax.axis_index("row")
    c = lax.axis_index("col")
    z = c // 2
    core = lax.rem(c, 2)
    width = noise.shape[1]
    height, depth = images.shape
    half = height // 2

    def at(row, col):
        return {"row": row, "col": col}

    partner = at(r, flip(c))
    up = at(r, lax.rem(c + 2, 2 * chips))
    down = at(r, lax.rem(c + 2 * chips - 2, 2 * chips))
    others = [lax.rem(r + k, rows) for k in range(1, rows)]
    greet(
        [(partner, None), (up, z < chips - 1), (down, z > 0)]
        + [(at(other, c), None) for other in others]
    )

    def noise_slot(chip, parity):
        if len(all_noise.shape) == 3:
            return all_noise.at[chip * 2 + parity]
        start = pl.multiple_of((chip * 2 + parity) * width, width)
        return all_noise.at[:, pl.ds(start, width)]

    def image_slot(owner, first, count):
        start = pl.multiple_of(owner * depth, depth)
        return all_images.at[pl.ds(first, count), pl.ds(start, depth)]

    def go_up(src, s):
        chip = z - s
        return remote(src, noise_slot(chip, core), right_send.at[s], right_recv.at[s], up)

    def go_down(src, s):
        chip = z + s
        return remote(src, noise_slot(chip, core), left_send.at[s], left_recv.at[s], down)

    def go_pair(src, chip):
        return remote(src, noise_slot(chip, core), pair_send.at[chip], pair_recv.at[chip], partner)

    own_noise = pltpu.make_async_copy(noise, noise_slot(z, core), own_sem.at[0])
    own_images = pltpu.make_async_copy(images, image_slot(r, 0, height), own_sem.at[1])

    pl.when(z < chips - 1)(lambda: go_up(noise, 0).start())
    pl.when(z > 0)(lambda: go_down(noise, 0).start())

    if rows == 4:
        xn = flip(r)
        yn = lax.rem(r + 2, 4)
        dg = flip(yn)
        to_x, to_y = at(xn, c), at(yn, c)

        def part(src_ref, owner, second, k, target):
            first = half if second else 0
            src = images.at[pl.ds(first, half), :] if src_ref is None else image_slot(owner, first, half)
            return remote(
                src, image_slot(owner, first, half), row_send.at[k], row_recv.at[k], target
            )

        first_x, first_y = part(None, r, False, 0, to_x), part(None, r, True, 1, to_y)
        second_x, second_y = part(None, r, True, 2, to_x), part(None, r, False, 3, to_y)
        first_x.start()
        first_y.start()
        second_x.start()
        second_y.start()
        pass_y, pass_x = part(0, xn, False, 4, to_y), part(0, yn, True, 5, to_x)
        in_first_x, in_first_y = part(None, xn, False, 0, to_x), part(None, yn, True, 1, to_y)
        in_second_x, in_second_y = part(None, xn, True, 2, to_x), part(None, yn, False, 3, to_y)
        in_pass_y, in_pass_x = part(None, dg, False, 4, to_y), part(None, dg, True, 5, to_x)
    else:
        sends = [
            remote(images, image_slot(r, 0, height), row_send.at[k], row_recv.at[k], at(other, c))
            for k, other in enumerate(others)
        ]
        for copy in sends:
            copy.start()

    own_noise.start()
    own_images.start()
    go_pair(noise, z).start()

    for s in range(chips - 1):
        from_down = z - 1 - s >= 0
        from_up = z + 1 + s < chips

        def arrived_up(s=s):
            chip = z - 1 - s
            remote(noise, noise_slot(chip, core), right_send.at[s], right_recv.at[s], up).wait_recv()
            if s + 1 < chips - 1:
                pl.when(z < chips - 1)(lambda: go_up(noise_slot(chip, core), s + 1).start())
            go_pair(noise_slot(chip, core), chip).start()

        def arrived_down(s=s):
            chip = z + 1 + s
            remote(noise, noise_slot(chip, core), left_send.at[s], left_recv.at[s], down).wait_recv()
            if s + 1 < chips - 1:
                pl.when(z > 0)(lambda: go_down(noise_slot(chip, core), s + 1).start())
            go_pair(noise_slot(chip, core), chip).start()

        pl.when(from_down)(arrived_up)
        pl.when(from_up)(arrived_down)
        if rows == 4 and s == min(1, chips - 2):
            in_first_x.wait_recv()
            pass_y.start()
            in_first_y.wait_recv()
            pass_x.start()

    if rows == 4:
        for copy in (in_second_x, in_second_y, in_pass_y, in_pass_x):
            copy.wait_recv()
        for copy in (first_x, first_y, second_x, second_y, pass_y, pass_x):
            copy.wait_send()
    else:
        for k, other in enumerate(others):
            source = lax.rem(r + rows - 1 - k, rows)
            remote(
                images, image_slot(source, 0, height), row_send.at[k], row_recv.at[k], at(other, c)
            ).wait_recv()
        for copy in sends:
            copy.wait_send()

    own_noise.wait()
    own_images.wait()
    for s in range(chips - 1):
        pl.when(jnp.logical_and(z < chips - 1, z - s >= 0))(lambda s=s: go_up(noise, s).wait_send())
        pl.when(jnp.logical_and(z > 0, z + s < chips))(lambda s=s: go_down(noise, s).wait_send())
    for chip in range(chips):
        copy = remote(
            noise, noise_slot(chip, 1 - core), pair_send.at[chip], pair_recv.at[chip], partner
        )
        copy.wait_send()
        copy.wait_recv()


def gathered(noise, images, rows, cols):
    chips = cols // 2
    dma = pltpu.SemaphoreType.DMA
    anywhere = pl.BlockSpec(memory_space=pl.ANY)
    inside = pl.BlockSpec(memory_space=pltpu.VMEM)
    steps = max(chips - 1, 1)
    points, width = noise.shape
    stacked = width % 128 != 0
    full_noise, full_images = pl.pallas_call(
        functools.partial(gather_kernel, rows, chips),
        out_shape=(
            jax.ShapeDtypeStruct(
                (cols, points, width) if stacked else (points, width * cols), jnp.float32
            ),
            jax.ShapeDtypeStruct((images.shape[0], images.shape[1] * rows), jnp.float32),
        ),
        in_specs=[inside, inside],
        out_specs=(anywhere, anywhere),
        scratch_shapes=[
            dma((2,)), dma((steps,)), dma((steps,)), dma((steps,)), dma((steps,)),
            dma((chips,)), dma((chips,)), dma((max(rows, 6),)), dma((max(rows, 6),)),
        ],
        compiler_params=params(0),
        name="gather",
    )(noise, images)
    if stacked:
        full_noise = jnp.swapaxes(full_noise, 0, 1).reshape(points, width * cols)
    return full_noise, full_images


def sinkhorn_kernel(
    rows, cols, noise_count, image_count, scaled, weights, row_out, col_out,
    row_mine, row_all, col_mine, col_all, stat_peak, stat_total, pots,
    row_send, row_recv, col_send, col_recv,
):
    r = lax.axis_index("row")
    c = lax.axis_index("col")
    points, pictures = scaled.shape
    slab = 64
    slabs = points // slab

    def at(row, col):
        return {"row": row, "col": col}

    row_peers = [at(r, lax.rem(c + k, cols)) for k in range(1, cols)]
    col_peers = [at(lax.rem(r + k, rows), c) for k in range(1, rows)]
    greet([(peer, None) for peer in row_peers + col_peers])

    def exchange(mine, everything, send, recv, peers, position, turn):
        count = len(peers) + 1
        copies = [
            remote(mine.at[turn], everything.at[turn, position], send.at[turn, k], recv.at[turn, k], peer)
            for k, peer in enumerate(peers)
        ]
        for copy in copies:
            copy.start()
        for k, peer in enumerate(peers):
            source = lax.rem(position + count - 1 - k, count)
            remote(
                mine.at[turn], everything.at[turn, source], send.at[turn, k], recv.at[turn, k], peer
            ).wait_recv()
        for copy in copies:
            copy.wait_send()
        peak, total = mine[turn, 0:1, :], mine[turn, 1:2, :]
        sources = [lax.rem(position + k, count) for k in range(1, count)]
        pairs = [everything[turn, source] for source in sources]
        top = peak
        for pair in pairs:
            top = jnp.maximum(top, pair[0:1])
        whole = total * jnp.exp(peak - top)
        for pair in pairs:
            whole = whole + pair[1:2] * jnp.exp(pair[0:1] - top)
        return jnp.log(whole) + top

    def over_images(col_pot, turn):
        def step(i, carry):
            window = pl.ds(pl.multiple_of(i * slab, slab), slab)
            logits = col_pot - scaled[window, :]
            peak = jnp.max(logits, axis=1, keepdims=True)
            total = jnp.sum(jnp.exp(logits - peak), axis=1, keepdims=True)
            stat_peak[window, :] = jnp.broadcast_to(peak, (slab, 128))
            stat_total[window, :] = jnp.broadcast_to(total, (slab, 128))
            return carry

        lax.fori_loop(0, slabs, step, 0)
        row_mine[turn, 0:1, :] = stat_peak[...].T[0:1, :]
        row_mine[turn, 1:2, :] = stat_total[...].T[0:1, :]
        return exchange(row_mine, row_all, row_send, row_recv, row_peers, c, turn)

    def as_column(line):
        pots[...] = jnp.broadcast_to(line, (128, points)).T

    def over_noise(turn):
        def top_of(i, peak):
            window = pl.ds(pl.multiple_of(i * slab, slab), slab)
            logits = pots[window, 0:1] - scaled[window, :]
            return jnp.maximum(peak, jnp.max(logits, axis=0, keepdims=True))

        peak = lax.fori_loop(0, slabs, top_of, jnp.full((1, pictures), -jnp.inf, jnp.float32))

        def sum_of(i, total):
            window = pl.ds(pl.multiple_of(i * slab, slab), slab)
            logits = pots[window, 0:1] - scaled[window, :]
            return total + jnp.sum(jnp.exp(logits - peak), axis=0, keepdims=True)

        total = lax.fori_loop(0, slabs, sum_of, jnp.zeros((1, pictures), jnp.float32))
        col_mine[turn, 0:1, :] = peak
        col_mine[turn, 1:2, :] = total
        return exchange(col_mine, col_all, col_send, col_recv, col_peers, r, turn)

    col_pot = jnp.zeros((1, pictures), jnp.float32)
    for turn in range(ITERS):
        row_pot = jnp.log(jnp.float32(image_count)) - over_images(col_pot, turn)
        as_column(row_pot)
        col_pot = jnp.log(jnp.float32(noise_count)) - over_noise(turn)
    row_out[...] = row_pot
    col_out[...] = col_pot
    as_column(over_images(col_pot, ITERS))

    def weigh(i, carry):
        window = pl.ds(pl.multiple_of(i * slab, slab), slab)
        weights[window, :] = jnp.exp(col_pot - scaled[window, :] - pots[window, 0:1])
        return carry

    lax.fori_loop(0, slabs, weigh, 0)


def coupled(scaled, rows, cols):
    points, pictures = scaled.shape
    dma = pltpu.SemaphoreType.DMA
    inside = pl.BlockSpec(memory_space=pltpu.VMEM)
    turns = ITERS + 1
    weights, row_pot, col_pot = pl.pallas_call(
        functools.partial(sinkhorn_kernel, rows, cols, points * rows, pictures * cols),
        out_shape=(
            jax.ShapeDtypeStruct((points, pictures), jnp.float32),
            jax.ShapeDtypeStruct((1, points), jnp.float32),
            jax.ShapeDtypeStruct((1, pictures), jnp.float32),
        ),
        in_specs=[inside],
        out_specs=(inside, inside, inside),
        scratch_shapes=[
            pltpu.VMEM((turns, 2, points), jnp.float32),
            pltpu.VMEM((turns, cols, 2, points), jnp.float32),
            pltpu.VMEM((ITERS, 2, pictures), jnp.float32),
            pltpu.VMEM((ITERS, rows, 2, pictures), jnp.float32),
            pltpu.VMEM((points, 128), jnp.float32),
            pltpu.VMEM((points, 128), jnp.float32),
            pltpu.VMEM((points, 128), jnp.float32),
            dma((turns, cols)), dma((turns, cols)), dma((ITERS, rows)), dma((ITERS, rows)),
        ],
        compiler_params=params(1),
        name="sinkhorn",
    )(scaled)
    return weights, row_pot[0], col_pot[0]


def total_kernel(
    chips, count, slack, part, whole, own, other, going, coming,
    load_sem, keep_sem, pair_send, pair_recv, sum_send, sum_recv,
    cast_send, cast_recv, share_send, share_recv,
):
    r = lax.axis_index("row")
    c = lax.axis_index("col")
    z = c // 2
    core = lax.rem(c, 2)
    points, features = part.shape
    width = features // 2
    tall = points // count
    per_way = count // 2
    last = chips - 1

    def at(col):
        return {"row": r, "col": col}

    partner = at(flip(c))
    up = at(lax.rem(c + 2, 2 * chips))
    down = at(lax.rem(c + 2 * chips - 2, 2 * chips))
    greet([(partner, None), (up, z < last), (down, z > 0)])

    mine = pl.multiple_of(core * width, width)
    theirs = pl.multiple_of((1 - core) * width, width)

    def rows_of(j):
        return pl.ds(pl.multiple_of(j * tall, tall), tall)

    def load(j):
        return pltpu.make_async_copy(
            part.at[rows_of(j), pl.ds(mine, width)], own.at[rows_of(j), :], load_sem.at[j]
        )

    def pair(j):
        return remote(
            part.at[rows_of(j), pl.ds(theirs, width)], other.at[rows_of(j), :],
            pair_send.at[j], pair_recv.at[j], partner,
        )

    def start(j, carry):
        pair(j).start()
        load(j).start()
        return carry

    lax.fori_loop(0, count, start, 0)

    def reduce_step(j, first, final, onward):
        load(j).wait()
        pair(j).wait_recv()
        window = rows_of(j)

        @pl.when(first)
        def _():
            going[window, :] = own[window, :] + other[window, :]

        @pl.when(jnp.logical_not(first))
        def _():
            hop(j, onward).wait_recv()
            going[window, :] = own[window, :] + other[window, :] + coming[window, :]

        @pl.when(jnp.logical_not(final))
        def _():
            hop(j, onward).start()

    def hop(j, target):
        return remote(
            going.at[rows_of(j), :], coming.at[rows_of(j), :], sum_send.at[j], sum_recv.at[j], target
        )

    def spot(j, start_col):
        return whole.at[rows_of(j), pl.ds(start_col, width)]

    def cast(j, target):
        return remote(spot(j, mine), spot(j, mine), cast_send.at[j], cast_recv.at[j], target)

    def cast_first(j, target):
        return remote(going.at[rows_of(j), :], spot(j, mine), cast_send.at[j], cast_recv.at[j], target)

    def share(j):
        return remote(spot(j, mine), spot(j, mine), share_send.at[j], share_recv.at[j], partner)

    def share_first(j):
        return remote(going.at[rows_of(j), :], spot(j, mine), share_send.at[j], share_recv.at[j], partner)

    def keep(j):
        return pltpu.make_async_copy(going.at[rows_of(j), :], spot(j, mine), keep_sem.at[j])

    def way(step, here, parity, onward, back):
        j = step - slack * here

        @pl.when(jnp.logical_and(j >= 0, j < per_way))
        def _():
            index = 2 * j + parity
            reduce_step(index, here == 0, here == last, onward)

            @pl.when(here == last)
            def _():
                cast_first(index, back).start()
                keep(index).start()
                share_first(index).start()

        k = step - slack * (2 * last - here)

        @pl.when(jnp.logical_and(jnp.logical_and(k >= 0, k < per_way), here < last))
        def _():
            index = 2 * k + parity
            cast(index, back).wait_recv()

            @pl.when(here > 0)
            def _():
                cast(index, back).start()

            share(index).start()

    def step(s, carry):
        way(s, z, 0, up, down)
        way(s, last - z, 1, down, up)
        return carry

    lax.fori_loop(0, per_way + slack * 2 * last, step, 0)

    def finish(j, carry):
        pair(j).wait_send()
        share(j).wait_send()
        remote(
            spot(j, mine), spot(j, theirs), share_send.at[j], share_recv.at[j], partner
        ).wait_recv()
        here = jnp.where(lax.rem(j, 2) == 0, z, last - z)

        @pl.when(here < last)
        def _():
            hop(j, partner).wait_send()

        @pl.when(here == last)
        def _():
            keep(j).wait()

        @pl.when(here > 0)
        def _():
            cast(j, partner).wait_send()

        return carry

    lax.fori_loop(0, count, finish, 0)


def total_over_col(part, cols, collective_id):
    points, features = part.shape
    chips = cols // 2
    count = points // TALL
    dma = pltpu.SemaphoreType.DMA
    anywhere = pl.BlockSpec(memory_space=pl.ANY)
    return pl.pallas_call(
        functools.partial(total_kernel, chips, count, SLACK),
        out_shape=jax.ShapeDtypeStruct((points, features), jnp.float32),
        in_specs=[anywhere],
        out_specs=anywhere,
        scratch_shapes=[pltpu.VMEM((points, features // 2), jnp.float32)] * 4 + [dma((count,))] * 10,
        compiler_params=params(collective_id),
        name=f"total{collective_id}",
    )(part)


def halves(x):
    high = x.astype(jnp.bfloat16)
    return high, (x - high.astype(jnp.float32)).astype(jnp.bfloat16)


def three_pass(left, right, dims):
    left_high, left_low = halves(left)
    right_high, right_low = halves(right)

    def product(a, b):
        return lax.dot_general(a, b, (dims, ((), ())), preferred_element_type=jnp.float32)

    return product(left_high, right_high) + (
        product(left_high, right_low) + product(left_low, right_high)
    )


class Scatter:
    def __init__(self, rows, r, c, piece, inbox, relay, send, recv):
        self.rows, self.r, self.c, self.piece = rows, r, c, piece
        self.inbox, self.relay, self.send, self.recv = inbox, relay, send, recv
        self.half = inbox.shape[1] // 2
        self.peers = [{"row": lax.rem(r + k, rows), "col": c} for k in range(1, rows)]
        if rows == 4:
            self.xn = flip(r)
            self.yn = lax.rem(r + 2, 4)
            self.dg = flip(self.yn)
            self.to_x = {"row": self.xn, "col": c}
            self.to_y = {"row": self.yn, "col": c}

    def copy(self, k):
        first, second = pl.ds(0, self.half), pl.ds(self.half, self.half)
        src, dst, target = (
            (lambda: self.piece(self.dg, first), self.relay.at[0], self.to_x),
            (lambda: self.piece(self.dg, second), self.relay.at[1], self.to_y),
            (lambda: self.piece(self.xn, first), self.inbox.at[0, first, :], self.to_x),
            (lambda: self.piece(self.yn, second), self.inbox.at[1, second, :], self.to_y),
            (lambda: self.relay.at[0], self.inbox.at[1, first, :], self.to_y),
            (lambda: self.relay.at[1], self.inbox.at[0, second, :], self.to_x),
        )[k]
        return remote(src(), dst, self.send.at[k], self.recv.at[k], target)

    def direct(self, k):
        owner = lax.rem(self.r + 1 + k, self.rows)
        return remote(
            self.piece(owner, pl.ds(0, 2 * self.half)), self.inbox.at[k],
            self.send.at[k], self.recv.at[k], self.peers[k],
        )

    def order(self):
        if self.rows == 4:
            return [self.dg, self.xn, self.yn, self.r]
        return [lax.rem(self.r + 1 + k, self.rows) for k in range(self.rows)]

    def ready(self, place):
        if self.rows == 4:
            for k in ((0, 1), (2,), (3,), ())[place]:
                self.copy(k).start()
        elif place < self.rows - 1:
            self.direct(place).start()

    def forward(self):
        if self.rows == 4:
            first, second = pl.ds(0, self.half), pl.ds(self.half, self.half)
            self.copy(0).wait_recv()
            self.relay[0] = self.relay[0] + self.piece(self.yn, first)[...]
            self.copy(4).start()
            self.copy(1).wait_recv()
            self.relay[1] = self.relay[1] + self.piece(self.xn, second)[...]
            self.copy(5).start()

    def finish(self, out):
        own = self.piece(self.r, pl.ds(0, 2 * self.half))
        if self.rows == 4:
            for k in (2, 3, 4, 5):
                self.copy(k).wait_recv()
            out[...] = own[...] + self.inbox[0] + self.inbox[1]
            for k in range(6):
                self.copy(k).wait_send()
        else:
            for k in range(self.rows - 1):
                self.direct(k).wait_recv()
            out[...] = own[...]
            for k in range(self.rows - 1):
                out[...] = out[...] + self.inbox[k]
            for k in range(self.rows - 1):
                self.direct(k).wait_send()


def backward_kernel(
    rows, fraction, pre, squared, local_out, slope, w_out, mixed, grad_in, grad_out, grad_time, error,
    local_out_in, slope_in, w_out_in, mixed_in, local_in, back,
    out_inbox, out_relay, in_inbox, in_relay, sums,
    load_sem, out_send, out_recv, in_send, in_recv, sum_send, sum_recv,
):
    r = lax.axis_index("row")
    c = lax.axis_index("col")
    hidden, features = local_out.shape
    block = features // rows
    peers = [{"row": lax.rem(r + k, rows), "col": c} for k in range(1, rows)]
    greet([(peer, None) for peer in peers])

    loads = [
        pltpu.make_async_copy(src, dst, load_sem.at[k])
        for k, (src, dst) in enumerate(
            ((local_out, local_out_in), (slope, slope_in), (w_out, w_out_in), (mixed, mixed_in))
        )
    ]
    for load in loads:
        load.start()

    def columns(owner):
        return pl.ds(pl.multiple_of(owner * block, block), block)

    def out_piece(owner, window):
        return local_out_in.at[window, columns(owner)]

    def in_piece(owner, window):
        start = pl.multiple_of(owner * block, block) + window.start
        return local_in.at[pl.ds(pl.multiple_of(start, 8), window.size), :]

    over_out = Scatter(rows, r, c, out_piece, out_inbox, out_relay, out_send, out_recv)
    over_in = Scatter(rows, r, c, in_piece, in_inbox, in_relay, in_send, in_recv)

    loads[0].wait()
    for place in range(rows):
        over_out.ready(place)

    loads[1].wait()
    loads[2].wait()
    back[...] = jnp.zeros_like(back)

    def back_step(k, carry):
        window = columns(k)
        back[...] += three_pass(slope_in[:, window], w_out_in[:, window], ((1,), (1,)))
        return carry

    lax.fori_loop(0, rows, back_step, 0)
    sigma = 1.0 / (1.0 + jnp.exp(-pre[...]))
    back[...] = back[...] * sigma * (1.0 + pre[...] * (1.0 - sigma))
    sums[r, 0:1, :] = jnp.sum(fraction[...] * back[...], axis=0, keepdims=True)
    sums[r, 1:2, :] = squared[...]

    def share(k, slot):
        return remote(sums.at[slot], sums.at[slot], sum_send.at[k], sum_recv.at[k], peers[k])

    for k in range(rows - 1):
        share(k, r).start()

    loads[3].wait()
    over_out.forward()
    order = over_in.order()
    for place in range(rows):
        owner = order[place]
        local_in[columns(owner), :] = three_pass(mixed_in[:, columns(owner)], back[...], ((0,), (0,)))
        over_in.ready(place)
        if place == rows - 2:
            over_in.forward()
    for k in range(rows - 1):
        share(k, lax.rem(r + rows - 1 - k, rows)).wait_recv()
    for k in range(rows - 1):
        share(k, r).wait_send()
    both = sums[0]
    for k in range(1, rows):
        both = both + sums[k]
    grad_time[...] = both[0:1]
    error[...] = both[1:2]
    over_out.finish(grad_out)
    over_in.finish(grad_in)


def gradients(fraction, pre, squared, local_out, slope, w_out, mixed, rows):
    points, hidden = pre.shape
    features = mixed.shape[1]
    block = features // rows
    dma = pltpu.SemaphoreType.DMA
    vmem = functools.partial(pltpu.VMEM, dtype=jnp.float32)
    anywhere = pl.BlockSpec(memory_space=pl.ANY)
    inside = pl.BlockSpec(memory_space=pltpu.VMEM)
    boxes = 2 if rows == 4 else rows - 1
    copies = max(rows, 6)

    def result(*shape):
        return jax.ShapeDtypeStruct(shape, jnp.float32)

    return pl.pallas_call(
        functools.partial(backward_kernel, rows),
        out_shape=(
            result(block, hidden), result(hidden, block), result(1, hidden), result(1, hidden),
        ),
        in_specs=[inside] * 3 + [anywhere] * 4,
        out_specs=(inside,) * 4,
        scratch_shapes=[
            vmem((hidden, features)), vmem((points, features)), vmem((hidden, features)),
            vmem((points, features)), vmem((features, hidden)), vmem((points, hidden)),
            vmem((boxes, hidden, block)), vmem((2, hidden // 2, block)),
            vmem((boxes, block, hidden)), vmem((2, block // 2, hidden)),
            vmem((rows, 2, hidden)),
            dma((4,)), dma((copies,)), dma((copies,)), dma((copies,)), dma((copies,)),
            dma((rows,)), dma((rows,)),
        ],
        compiler_params=params(4),
        name="backward",
    )(
        fraction[:, None], pre, jnp.broadcast_to(squared, (1, hidden)), local_out, slope, w_out, mixed
    )


def body(rows, cols, noise, images, time_index, w_in, time_gain, w_out):
    high = lax.Precision.HIGH
    full_noise, full_images = gathered(noise, images, rows, cols)
    width = full_noise.shape[1]
    noise_count = full_noise.shape[0] * rows
    noise_norms = jnp.sum(full_noise * full_noise, axis=1)
    image_norms = jnp.sum(full_images * full_images, axis=1)
    cross = lax.dot_general(
        full_noise,
        full_images,
        (((1,), (1,)), ((), ())),
        precision=high,
        preferred_element_type=jnp.float32,
    )
    scaled = (noise_norms[:, None] + image_norms[None, :] - 2.0 * cross) / (width * EPSILON)
    weights, row_pot, col_pot = coupled(scaled, rows, cols)
    partial_value = jnp.dot(
        weights, full_images, precision=high, preferred_element_type=jnp.float32
    )
    slice_width = noise.shape[1]
    slice_start = lax.axis_index("col") * slice_width
    whole_targets = total_over_col(partial_value, cols, 2)
    targets = lax.dynamic_slice_in_dim(whole_targets, slice_start, slice_width, 1)
    fraction = (time_index.astype(jnp.float32) + 0.5) / TIMES
    mixed = (1.0 - fraction)[:, None] * full_noise + fraction[:, None] * whole_targets
    velocity = whole_targets - full_noise
    pre = (
        jnp.dot(mixed, w_in, precision=high, preferred_element_type=jnp.float32)
        + fraction[:, None] * time_gain[None, :]
    )
    sigma = jax.nn.sigmoid(pre)
    hidden = pre * sigma
    part_out = jnp.dot(hidden, w_out, precision=high, preferred_element_type=jnp.float32)
    out = total_over_col(part_out, cols, 3)
    diff = out - velocity
    squared = jnp.sum(diff * diff)
    slope = diff / jnp.sqrt(jnp.float32(noise_count))
    local_out = lax.dot_general(
        hidden,
        slope,
        (((0,), (0,)), ((), ())),
        precision=high,
        preferred_element_type=jnp.float32,
    )
    grad_in, grad_out, grad_time, squared_all = gradients(
        fraction, pre, squared, local_out, slope, w_out, mixed, rows
    )
    mse = squared_all[0, 0] / (noise_count * width)
    return (targets, row_pot, col_pot, grad_in, grad_time[0], grad_out, mse)


def solution(mesh):
    placed = (P("row", "col"), P("col", "row"), P("row"), P(None, "col"), P("col"), P("col", None))
    return jax.shard_map(
        functools.partial(body, mesh.shape["row"], mesh.shape["col"]),
        mesh=mesh,
        in_specs=placed,
        out_specs=(
            P("row", "col"),
            P("row"),
            P("col"),
            P("row", "col"),
            P("col"),
            P("col", "row"),
            P(),
        ),
        check_vma=False,
    )
```

```python
import functools

import jax
import jax.numpy as jnp
from jax import lax
from jax.experimental import pallas as pl
from jax.experimental.pallas import tpu as pltpu
from jax.sharding import PartitionSpec as P

ITERS = 2
TIMES = 1000


EPSILON = 0.01
TALL = 16
SLACK = 2
MESH = pl.DeviceIdType.MESH
VMEM_LIMIT = 60 * 1024 * 1024


def params(collective_id):
    return pltpu.CompilerParams(
        collective_id=collective_id, has_side_effects=True, vmem_limit_bytes=VMEM_LIMIT
    )


def remote(src, dst, send_sem, recv_sem, device):
    return pltpu.make_async_remote_copy(
        src_ref=src,
        dst_ref=dst,
        send_sem=send_sem,
        recv_sem=recv_sem,
        device_id=device,
        device_id_type=MESH,
    )


def flip(index):
    return index + 1 - 2 * lax.rem(index, 2)


def greet(devices):
    barrier = pltpu.get_barrier_semaphore()
    for device, condition in devices:
        def signal(device=device):
            pl.semaphore_signal(barrier, inc=1, device_id=device, device_id_type=MESH)
        if condition is None:
            signal()
        else:
            pl.when(condition)(signal)
    count = jnp.int32(0)
    for device, condition in devices:
        count = count + (1 if condition is None else jnp.where(condition, 1, 0))
    pl.semaphore_wait(barrier, count)


def gather_kernel(
    rows, chips, noise, images, all_noise, all_images,
    own_sem, right_send, right_recv, left_send, left_recv, pair_send, pair_recv, row_send, row_recv,
):
    r = lax.axis_index("row")
    c = lax.axis_index("col")
    z = c // 2
    core = lax.rem(c, 2)
    width = noise.shape[1]
    height, depth = images.shape
    half = height // 2

    def at(row, col):
        return {"row": row, "col": col}

    partner = at(r, flip(c))
    up = at(r, lax.rem(c + 2, 2 * chips))
    down = at(r, lax.rem(c + 2 * chips - 2, 2 * chips))
    others = [lax.rem(r + k, rows) for k in range(1, rows)]
    greet(
        [(partner, None), (up, z < chips - 1), (down, z > 0)]
        + [(at(other, c), None) for other in others]
    )

    def noise_slot(chip, parity):
        if len(all_noise.shape) == 3:
            return all_noise.at[chip * 2 + parity]
        start = pl.multiple_of((chip * 2 + parity) * width, width)
        return all_noise.at[:, pl.ds(start, width)]

    def image_slot(owner, first, count):
        start = pl.multiple_of(owner * depth, depth)
        return all_images.at[pl.ds(first, count), pl.ds(start, depth)]

    def go_up(src, s):
        chip = z - s
        return remote(src, noise_slot(chip, core), right_send.at[s], right_recv.at[s], up)

    def go_down(src, s):
        chip = z + s
        return remote(src, noise_slot(chip, core), left_send.at[s], left_recv.at[s], down)

    def go_pair(src, chip):
        return remote(src, noise_slot(chip, core), pair_send.at[chip], pair_recv.at[chip], partner)

    own_noise = pltpu.make_async_copy(noise, noise_slot(z, core), own_sem.at[0])
    own_images = pltpu.make_async_copy(images, image_slot(r, 0, height), own_sem.at[1])

    pl.when(z < chips - 1)(lambda: go_up(noise, 0).start())
    pl.when(z > 0)(lambda: go_down(noise, 0).start())

    if rows == 4:
        xn = flip(r)
        yn = lax.rem(r + 2, 4)
        dg = flip(yn)
        to_x, to_y = at(xn, c), at(yn, c)

        def part(src_ref, owner, second, k, target):
            first = half if second else 0
            src = images.at[pl.ds(first, half), :] if src_ref is None else image_slot(owner, first, half)
            return remote(
                src, image_slot(owner, first, half), row_send.at[k], row_recv.at[k], target
            )

        first_x, first_y = part(None, r, False, 0, to_x), part(None, r, True, 1, to_y)
        second_x, second_y = part(None, r, True, 2, to_x), part(None, r, False, 3, to_y)
        first_x.start()
        first_y.start()
        second_x.start()
        second_y.start()
        pass_y, pass_x = part(0, xn, False, 4, to_y), part(0, yn, True, 5, to_x)
        in_first_x, in_first_y = part(None, xn, False, 0, to_x), part(None, yn, True, 1, to_y)
        in_second_x, in_second_y = part(None, xn, True, 2, to_x), part(None, yn, False, 3, to_y)
        in_pass_y, in_pass_x = part(None, dg, False, 4, to_y), part(None, dg, True, 5, to_x)
    else:
        sends = [
            remote(images, image_slot(r, 0, height), row_send.at[k], row_recv.at[k], at(other, c))
            for k, other in enumerate(others)
        ]
        for copy in sends:
            copy.start()

    own_noise.start()
    own_images.start()
    go_pair(noise, z).start()

    for s in range(chips - 1):
        from_down = z - 1 - s >= 0
        from_up = z + 1 + s < chips

        def arrived_up(s=s):
            chip = z - 1 - s
            remote(noise, noise_slot(chip, core), right_send.at[s], right_recv.at[s], up).wait_recv()
            if s + 1 < chips - 1:
                pl.when(z < chips - 1)(lambda: go_up(noise_slot(chip, core), s + 1).start())
            go_pair(noise_slot(chip, core), chip).start()

        def arrived_down(s=s):
            chip = z + 1 + s
            remote(noise, noise_slot(chip, core), left_send.at[s], left_recv.at[s], down).wait_recv()
            if s + 1 < chips - 1:
                pl.when(z > 0)(lambda: go_down(noise_slot(chip, core), s + 1).start())
            go_pair(noise_slot(chip, core), chip).start()

        pl.when(from_down)(arrived_up)
        pl.when(from_up)(arrived_down)
        if rows == 4 and s == min(1, chips - 2):
            in_first_x.wait_recv()
            pass_y.start()
            in_first_y.wait_recv()
            pass_x.start()

    if rows == 4:
        for copy in (in_second_x, in_second_y, in_pass_y, in_pass_x):
            copy.wait_recv()
        for copy in (first_x, first_y, second_x, second_y, pass_y, pass_x):
            copy.wait_send()
    else:
        for k, other in enumerate(others):
            source = lax.rem(r + rows - 1 - k, rows)
            remote(
                images, image_slot(source, 0, height), row_send.at[k], row_recv.at[k], at(other, c)
            ).wait_recv()
        for copy in sends:
            copy.wait_send()

    own_noise.wait()
    own_images.wait()
    for s in range(chips - 1):
        pl.when(jnp.logical_and(z < chips - 1, z - s >= 0))(lambda s=s: go_up(noise, s).wait_send())
        pl.when(jnp.logical_and(z > 0, z + s < chips))(lambda s=s: go_down(noise, s).wait_send())
    for chip in range(chips):
        copy = remote(
            noise, noise_slot(chip, 1 - core), pair_send.at[chip], pair_recv.at[chip], partner
        )
        copy.wait_send()
        copy.wait_recv()


def gathered(noise, images, rows, cols):
    chips = cols // 2
    dma = pltpu.SemaphoreType.DMA
    anywhere = pl.BlockSpec(memory_space=pl.ANY)
    inside = pl.BlockSpec(memory_space=pltpu.VMEM)
    steps = max(chips - 1, 1)
    points, width = noise.shape
    stacked = width % 128 != 0
    full_noise, full_images = pl.pallas_call(
        functools.partial(gather_kernel, rows, chips),
        out_shape=(
            jax.ShapeDtypeStruct(
                (cols, points, width) if stacked else (points, width * cols), jnp.float32
            ),
            jax.ShapeDtypeStruct((images.shape[0], images.shape[1] * rows), jnp.float32),
        ),
        in_specs=[inside, inside],
        out_specs=(anywhere, anywhere),
        scratch_shapes=[
            dma((2,)), dma((steps,)), dma((steps,)), dma((steps,)), dma((steps,)),
            dma((chips,)), dma((chips,)), dma((max(rows, 6),)), dma((max(rows, 6),)),
        ],
        compiler_params=params(0),
        name="gather",
    )(noise, images)
    if stacked:
        full_noise = jnp.swapaxes(full_noise, 0, 1).reshape(points, width * cols)
    return full_noise, full_images


def sinkhorn_kernel(
    rows, cols, noise_count, image_count, scaled, weights, row_out, col_out,
    row_mine, row_all, col_mine, col_all, stat_peak, stat_total, pots,
    row_send, row_recv, col_send, col_recv,
):
    r = lax.axis_index("row")
    c = lax.axis_index("col")
    points, pictures = scaled.shape
    slab = 64
    slabs = points // slab

    def at(row, col):
        return {"row": row, "col": col}

    row_peers = [at(r, lax.rem(c + k, cols)) for k in range(1, cols)]
    col_peers = [at(lax.rem(r + k, rows), c) for k in range(1, rows)]
    greet([(peer, None) for peer in row_peers + col_peers])

    def exchange(mine, everything, send, recv, peers, position, turn):
        count = len(peers) + 1
        copies = [
            remote(mine.at[turn], everything.at[turn, position], send.at[turn, k], recv.at[turn, k], peer)
            for k, peer in enumerate(peers)
        ]
        for copy in copies:
            copy.start()
        for k, peer in enumerate(peers):
            source = lax.rem(position + count - 1 - k, count)
            remote(
                mine.at[turn], everything.at[turn, source], send.at[turn, k], recv.at[turn, k], peer
            ).wait_recv()
        for copy in copies:
            copy.wait_send()
        peak, total = mine[turn, 0:1, :], mine[turn, 1:2, :]
        sources = [lax.rem(position + k, count) for k in range(1, count)]
        pairs = [everything[turn, source] for source in sources]
        top = peak
        for pair in pairs:
            top = jnp.maximum(top, pair[0:1])
        whole = total * jnp.exp(peak - top)
        for pair in pairs:
            whole = whole + pair[1:2] * jnp.exp(pair[0:1] - top)
        return jnp.log(whole) + top

    def over_images(col_pot, turn):
        def step(i, carry):
            window = pl.ds(pl.multiple_of(i * slab, slab), slab)
            logits = col_pot - scaled[window, :]
            peak = jnp.max(logits, axis=1, keepdims=True)
            total = jnp.sum(jnp.exp(logits - peak), axis=1, keepdims=True)
            stat_peak[window, :] = jnp.broadcast_to(peak, (slab, 128))
            stat_total[window, :] = jnp.broadcast_to(total, (slab, 128))
            return carry

        lax.fori_loop(0, slabs, step, 0)
        row_mine[turn, 0:1, :] = stat_peak[...].T[0:1, :]
        row_mine[turn, 1:2, :] = stat_total[...].T[0:1, :]
        return exchange(row_mine, row_all, row_send, row_recv, row_peers, c, turn)

    def as_column(line):
        pots[...] = jnp.broadcast_to(line, (128, points)).T

    def over_noise(turn):
        def top_of(i, peak):
            window = pl.ds(pl.multiple_of(i * slab, slab), slab)
            logits = pots[window, 0:1] - scaled[window, :]
            return jnp.maximum(peak, jnp.max(logits, axis=0, keepdims=True))

        peak = lax.fori_loop(0, slabs, top_of, jnp.full((1, pictures), -jnp.inf, jnp.float32))

        def sum_of(i, total):
            window = pl.ds(pl.multiple_of(i * slab, slab), slab)
            logits = pots[window, 0:1] - scaled[window, :]
            return total + jnp.sum(jnp.exp(logits - peak), axis=0, keepdims=True)

        total = lax.fori_loop(0, slabs, sum_of, jnp.zeros((1, pictures), jnp.float32))
        col_mine[turn, 0:1, :] = peak
        col_mine[turn, 1:2, :] = total
        return exchange(col_mine, col_all, col_send, col_recv, col_peers, r, turn)

    col_pot = jnp.zeros((1, pictures), jnp.float32)
    for turn in range(ITERS):
        row_pot = jnp.log(jnp.float32(image_count)) - over_images(col_pot, turn)
        as_column(row_pot)
        col_pot = jnp.log(jnp.float32(noise_count)) - over_noise(turn)
    row_out[...] = row_pot
    col_out[...] = col_pot
    as_column(over_images(col_pot, ITERS))

    def weigh(i, carry):
        window = pl.ds(pl.multiple_of(i * slab, slab), slab)
        weights[window, :] = jnp.exp(col_pot - scaled[window, :] - pots[window, 0:1])
        return carry

    lax.fori_loop(0, slabs, weigh, 0)


def coupled(scaled, rows, cols):
    points, pictures = scaled.shape
    dma = pltpu.SemaphoreType.DMA
    inside = pl.BlockSpec(memory_space=pltpu.VMEM)
    turns = ITERS + 1
    weights, row_pot, col_pot = pl.pallas_call(
        functools.partial(sinkhorn_kernel, rows, cols, points * rows, pictures * cols),
        out_shape=(
            jax.ShapeDtypeStruct((points, pictures), jnp.float32),
            jax.ShapeDtypeStruct((1, points), jnp.float32),
            jax.ShapeDtypeStruct((1, pictures), jnp.float32),
        ),
        in_specs=[inside],
        out_specs=(inside, inside, inside),
        scratch_shapes=[
            pltpu.VMEM((turns, 2, points), jnp.float32),
            pltpu.VMEM((turns, cols, 2, points), jnp.float32),
            pltpu.VMEM((ITERS, 2, pictures), jnp.float32),
            pltpu.VMEM((ITERS, rows, 2, pictures), jnp.float32),
            pltpu.VMEM((points, 128), jnp.float32),
            pltpu.VMEM((points, 128), jnp.float32),
            pltpu.VMEM((points, 128), jnp.float32),
            dma((turns, cols)), dma((turns, cols)), dma((ITERS, rows)), dma((ITERS, rows)),
        ],
        compiler_params=params(1),
        name="sinkhorn",
    )(scaled)
    return weights, row_pot[0], col_pot[0]


def total_kernel(
    chips, count, slack, part, whole, own, other, going, coming,
    load_sem, keep_sem, pair_send, pair_recv, sum_send, sum_recv,
    cast_send, cast_recv, share_send, share_recv,
):
    r = lax.axis_index("row")
    c = lax.axis_index("col")
    z = c // 2
    core = lax.rem(c, 2)
    points, features = part.shape
    width = features // 2
    tall = points // count
    per_way = count // 2
    last = chips - 1

    def at(col):
        return {"row": r, "col": col}

    partner = at(flip(c))
    up = at(lax.rem(c + 2, 2 * chips))
    down = at(lax.rem(c + 2 * chips - 2, 2 * chips))
    greet([(partner, None), (up, z < last), (down, z > 0)])

    mine = pl.multiple_of(core * width, width)
    theirs = pl.multiple_of((1 - core) * width, width)

    def rows_of(j):
        return pl.ds(pl.multiple_of(j * tall, tall), tall)

    def load(j):
        return pltpu.make_async_copy(
            part.at[rows_of(j), pl.ds(mine, width)], own.at[rows_of(j), :], load_sem.at[j]
        )

    def pair(j):
        return remote(
            part.at[rows_of(j), pl.ds(theirs, width)], other.at[rows_of(j), :],
            pair_send.at[j], pair_recv.at[j], partner,
        )

    def start(j, carry):
        pair(j).start()
        load(j).start()
        return carry

    lax.fori_loop(0, count, start, 0)

    def reduce_step(j, first, final, onward):
        load(j).wait()
        pair(j).wait_recv()
        window = rows_of(j)

        @pl.when(first)
        def _():
            going[window, :] = own[window, :] + other[window, :]

        @pl.when(jnp.logical_not(first))
        def _():
            hop(j, onward).wait_recv()
            going[window, :] = own[window, :] + other[window, :] + coming[window, :]

        @pl.when(jnp.logical_not(final))
        def _():
            hop(j, onward).start()

    def hop(j, target):
        return remote(
            going.at[rows_of(j), :], coming.at[rows_of(j), :], sum_send.at[j], sum_recv.at[j], target
        )

    def spot(j, start_col):
        return whole.at[rows_of(j), pl.ds(start_col, width)]

    def cast(j, target):
        return remote(spot(j, mine), spot(j, mine), cast_send.at[j], cast_recv.at[j], target)

    def cast_first(j, target):
        return remote(going.at[rows_of(j), :], spot(j, mine), cast_send.at[j], cast_recv.at[j], target)

    def share(j):
        return remote(spot(j, mine), spot(j, mine), share_send.at[j], share_recv.at[j], partner)

    def share_first(j):
        return remote(going.at[rows_of(j), :], spot(j, mine), share_send.at[j], share_recv.at[j], partner)

    def keep(j):
        return pltpu.make_async_copy(going.at[rows_of(j), :], spot(j, mine), keep_sem.at[j])

    def way(step, here, parity, onward, back):
        j = step - slack * here

        @pl.when(jnp.logical_and(j >= 0, j < per_way))
        def _():
            index = 2 * j + parity
            reduce_step(index, here == 0, here == last, onward)

            @pl.when(here == last)
            def _():
                cast_first(index, back).start()
                keep(index).start()
                share_first(index).start()

        k = step - slack * (2 * last - here)

        @pl.when(jnp.logical_and(jnp.logical_and(k >= 0, k < per_way), here < last))
        def _():
            index = 2 * k + parity
            cast(index, back).wait_recv()

            @pl.when(here > 0)
            def _():
                cast(index, back).start()

            share(index).start()

    def step(s, carry):
        way(s, z, 0, up, down)
        way(s, last - z, 1, down, up)
        return carry

    lax.fori_loop(0, per_way + slack * 2 * last, step, 0)

    def finish(j, carry):
        pair(j).wait_send()
        share(j).wait_send()
        remote(
            spot(j, mine), spot(j, theirs), share_send.at[j], share_recv.at[j], partner
        ).wait_recv()
        here = jnp.where(lax.rem(j, 2) == 0, z, last - z)

        @pl.when(here < last)
        def _():
            hop(j, partner).wait_send()

        @pl.when(here == last)
        def _():
            keep(j).wait()

        @pl.when(here > 0)
        def _():
            cast(j, partner).wait_send()

        return carry

    lax.fori_loop(0, count, finish, 0)


def total_over_col(part, cols, collective_id):
    points, features = part.shape
    chips = cols // 2
    count = points // TALL
    dma = pltpu.SemaphoreType.DMA
    anywhere = pl.BlockSpec(memory_space=pl.ANY)
    return pl.pallas_call(
        functools.partial(total_kernel, chips, count, SLACK),
        out_shape=jax.ShapeDtypeStruct((points, features), jnp.float32),
        in_specs=[anywhere],
        out_specs=anywhere,
        scratch_shapes=[pltpu.VMEM((points, features // 2), jnp.float32)] * 4 + [dma((count,))] * 10,
        compiler_params=params(collective_id),
        name=f"total{collective_id}",
    )(part)


def halves(x):
    high = x.astype(jnp.bfloat16)
    return high, (x - high.astype(jnp.float32)).astype(jnp.bfloat16)


def three_pass(left, right, dims):
    left_high, left_low = halves(left)
    right_high, right_low = halves(right)

    def product(a, b):
        return lax.dot_general(a, b, (dims, ((), ())), preferred_element_type=jnp.float32)

    return product(left_high, right_high) + (
        product(left_high, right_low) + product(left_low, right_high)
    )


class Scatter:
    def __init__(self, rows, r, c, piece, inbox, relay, send, recv):
        self.rows, self.r, self.c, self.piece = rows, r, c, piece
        self.inbox, self.relay, self.send, self.recv = inbox, relay, send, recv
        self.half = inbox.shape[1] // 2
        self.peers = [{"row": lax.rem(r + k, rows), "col": c} for k in range(1, rows)]
        if rows == 4:
            self.xn = flip(r)
            self.yn = lax.rem(r + 2, 4)
            self.dg = flip(self.yn)
            self.to_x = {"row": self.xn, "col": c}
            self.to_y = {"row": self.yn, "col": c}

    def copy(self, k):
        first, second = pl.ds(0, self.half), pl.ds(self.half, self.half)
        src, dst, target = (
            (lambda: self.piece(self.dg, first), self.relay.at[0], self.to_x),
            (lambda: self.piece(self.dg, second), self.relay.at[1], self.to_y),
            (lambda: self.piece(self.xn, first), self.inbox.at[0, first, :], self.to_x),
            (lambda: self.piece(self.yn, second), self.inbox.at[1, second, :], self.to_y),
            (lambda: self.relay.at[0], self.inbox.at[1, first, :], self.to_y),
            (lambda: self.relay.at[1], self.inbox.at[0, second, :], self.to_x),
        )[k]
        return remote(src(), dst, self.send.at[k], self.recv.at[k], target)

    def direct(self, k):
        owner = lax.rem(self.r + 1 + k, self.rows)
        return remote(
            self.piece(owner, pl.ds(0, 2 * self.half)), self.inbox.at[k],
            self.send.at[k], self.recv.at[k], self.peers[k],
        )

    def order(self):
        if self.rows == 4:
            return [self.dg, self.xn, self.yn, self.r]
        return [lax.rem(self.r + 1 + k, self.rows) for k in range(self.rows)]

    def ready(self, place):
        if self.rows == 4:
            for k in ((0, 1), (2,), (3,), ())[place]:
                self.copy(k).start()
        elif place < self.rows - 1:
            self.direct(place).start()

    def forward(self):
        if self.rows == 4:
            first, second = pl.ds(0, self.half), pl.ds(self.half, self.half)
            self.copy(0).wait_recv()
            self.relay[0] = self.relay[0] + self.piece(self.yn, first)[...]
            self.copy(4).start()
            self.copy(1).wait_recv()
            self.relay[1] = self.relay[1] + self.piece(self.xn, second)[...]
            self.copy(5).start()

    def ready_for(self, owner):
        if self.rows == 4:
            @pl.when(self.dg == owner)
            def _():
                self.copy(0).start()
                self.copy(1).start()

            pl.when(self.xn == owner)(lambda: self.copy(2).start())
            pl.when(self.yn == owner)(lambda: self.copy(3).start())
        else:
            for k in range(self.rows - 1):
                pl.when(lax.rem(self.r + 1 + k, self.rows) == owner)(lambda k=k: self.direct(k).start())

    def forward_for(self, owner):
        if self.rows == 4:
            first, second = pl.ds(0, self.half), pl.ds(self.half, self.half)

            @pl.when(self.yn == owner)
            def _():
                self.copy(0).wait_recv()
                self.relay[0] = self.relay[0] + self.piece(self.yn, first)[...]
                self.copy(4).start()

            @pl.when(self.xn == owner)
            def _():
                self.copy(1).wait_recv()
                self.relay[1] = self.relay[1] + self.piece(self.xn, second)[...]
                self.copy(5).start()

    def finish(self, out):
        own = self.piece(self.r, pl.ds(0, 2 * self.half))
        if self.rows == 4:
            for k in (2, 3, 4, 5):
                self.copy(k).wait_recv()
            out[...] = own[...] + self.inbox[0] + self.inbox[1]
            for k in range(6):
                self.copy(k).wait_send()
        else:
            for k in range(self.rows - 1):
                self.direct(k).wait_recv()
            out[...] = own[...]
            for k in range(self.rows - 1):
                out[...] = out[...] + self.inbox[k]
            for k in range(self.rows - 1):
                self.direct(k).wait_send()


def backward_kernel(
    rows, chips, count, slack, scale, fraction, pre, part, velocity, w_out, mixed,
    grad_in, grad_out, grad_time, error,
    own, other, coming, whole, local_out, held, w_out_in, local_in, back, squares,
    out_inbox, out_relay, in_inbox, in_relay, sums,
    load_sem, pair_send, pair_recv, sum_send, sum_recv, cast_send, cast_recv, share_send, share_recv,
    held_sem, w_sem, out_send, out_recv, in_send, in_recv, small_send, small_recv,
):
    r = lax.axis_index("row")
    c = lax.axis_index("col")
    z = c // 2
    core = lax.rem(c, 2)
    points, features = part.shape
    block = features // rows
    per_block = count // rows
    per_way = count // 2
    half = points // 2
    tall = half // per_block
    last = chips - 1

    def at(col):
        return {"row": r, "col": col}

    partner = at(flip(c))
    up = at(lax.rem(c + 2, 2 * chips))
    down = at(lax.rem(c + 2 * chips - 2, 2 * chips))
    peers = [{"row": lax.rem(r + k, rows), "col": c} for k in range(1, rows)]
    greet([(partner, None), (up, z < last), (down, z > 0)] + [(peer, None) for peer in peers])

    def columns(owner):
        return pl.ds(pl.multiple_of(owner * block, block), block)

    def fixed(owner):
        return pl.ds(owner * block, block)

    def local(ref, j):
        start = pl.multiple_of(lax.rem(j, per_block) * tall, tall)
        return ref.at[pl.ds(start, tall), columns(j // per_block)]

    def spot(ref, j, which):
        start = pl.multiple_of(which * half + lax.rem(j, per_block) * tall, tall)
        return ref.at[pl.ds(start, tall), columns(j // per_block)]

    def load(j):
        return pltpu.make_async_copy(spot(part, j, core), local(own, j), load_sem.at[j])

    def pair(j):
        return remote(
            spot(part, j, 1 - core), local(other, j), pair_send.at[j], pair_recv.at[j], partner
        )

    def hop(j, target):
        return remote(local(own, j), local(coming, j), sum_send.at[j], sum_recv.at[j], target)

    def cast(j, target, src=None):
        src = spot(whole, j, core) if src is None else src
        return remote(src, spot(whole, j, core), cast_send.at[j], cast_recv.at[j], target)

    def share(j, src=None):
        src = spot(whole, j, core) if src is None else src
        return remote(src, spot(whole, j, core), share_send.at[j], share_recv.at[j], partner)

    def begin(j, carry):
        pair(j).start()
        load(j).start()
        return carry

    lax.fori_loop(0, count, begin, 0)

    def hold(source, owner):
        return pltpu.make_async_copy(
            source.at[:, fixed(owner)], held.at[:, fixed(owner)], held_sem.at[owner]
        )

    for owner in range(rows):
        hold(velocity, owner).start()
    w_load = pltpu.make_async_copy(w_out, w_out_in, w_sem.at[0])
    w_load.start()

    def way(step, here, parity, onward, behind):
        j = step - slack * here

        @pl.when(jnp.logical_and(j >= 0, j < per_way))
        def _():
            index = 2 * j + parity
            load(index).wait()
            pair(index).wait_recv()
            mine = local(own, index)

            @pl.when(here == 0)
            def _():
                mine[...] = mine[...] + local(other, index)[...]

            @pl.when(here > 0)
            def _():
                hop(index, onward).wait_recv()
                mine[...] = mine[...] + local(other, index)[...] + local(coming, index)[...]

            @pl.when(here < last)
            def _():
                hop(index, onward).start()

            @pl.when(here == last)
            def _():
                cast(index, behind, mine).start()
                share(index, mine).start()
                spot(whole, index, core)[...] = mine[...]

        k = step - slack * (2 * last - here)

        @pl.when(jnp.logical_and(jnp.logical_and(k >= 0, k < per_way), here < last))
        def _():
            index = 2 * k + parity
            cast(index, behind).wait_recv()

            @pl.when(here > 0)
            def _():
                cast(index, behind).start()

            share(index).start()

    def step(s, carry):
        way(s, z, 0, up, down)
        way(s, last - z, 1, down, up)
        return carry

    def out_piece(owner, window):
        return local_out.at[window, columns(owner)]

    def in_piece(owner, window):
        start = pl.multiple_of(owner * block, block) + window.start
        return local_in.at[pl.ds(pl.multiple_of(start, 8), window.size), :]

    over_out = Scatter(rows, r, c, out_piece, out_inbox, out_relay, out_send, out_recv)
    over_in = Scatter(rows, r, c, in_piece, in_inbox, in_relay, in_send, in_recv)

    sigma = 1.0 / (1.0 + jnp.exp(-pre[...]))
    back[...] = jnp.zeros_like(back)
    squares[...] = jnp.zeros_like(squares)
    done = 0
    for owner in range(rows):
        until = per_block // 2 * (owner + 1) + slack * 2 * last
        lax.fori_loop(done, until, step, 0)
        done = until

        def shared(i, carry, owner=owner):
            j = owner * per_block + i
            remote(
                spot(whole, j, core), spot(whole, j, 1 - core), share_send.at[j], share_recv.at[j], partner
            ).wait_recv()
            return carry

        lax.fori_loop(0, per_block, shared, 0)
        hold(velocity, owner).wait()
        diff = whole[:, fixed(owner)] - held[:, fixed(owner)]
        squares[...] += jnp.sum(diff * diff, axis=0, keepdims=True)
        slope = diff * scale
        hold(mixed, owner).start()
        hidden = pre[...] * (1.0 / (1.0 + jnp.exp(-pre[...])))
        local_out[:, fixed(owner)] = three_pass(hidden, slope, ((0,), (0,)))
        over_out.ready_for(owner)
        if owner == 0:
            w_load.wait()
        back[...] += three_pass(slope, w_out_in[:, fixed(owner)], ((1,), (1,)))
        if owner > 0:
            over_out.forward_for(owner - 1)

    back[...] = back[...] * sigma * (1.0 + pre[...] * (1.0 - sigma))
    sums[r, 0:1, :] = jnp.sum(fraction[...] * back[...], axis=0, keepdims=True)
    total = jnp.sum(squares[...], axis=1, keepdims=True)
    sums[r, 1:2, :] = jnp.broadcast_to(total, (1, back.shape[1]))

    def small(k, slot):
        return remote(sums.at[slot], sums.at[slot], small_send.at[k], small_recv.at[k], peers[k])

    for k in range(rows - 1):
        small(k, r).start()
    for owner in range(rows):
        hold(mixed, owner).wait()
    order = over_in.order()
    for place in range(rows):
        owner = order[place]
        local_in[columns(owner), :] = three_pass(held[:, columns(owner)], back[...], ((0,), (0,)))
        over_in.ready(place)
        if place == 0:
            over_out.forward_for(rows - 1)
        if place == rows - 2:
            over_in.forward()
    for k in range(rows - 1):
        small(k, lax.rem(r + rows - 1 - k, rows)).wait_recv()
    for k in range(rows - 1):
        small(k, r).wait_send()
    both = sums[0]
    for k in range(1, rows):
        both = both + sums[k]
    grad_time[...] = both[0:1]
    error[...] = both[1:2]

    def finish(j, carry):
        pair(j).wait_send()
        share(j).wait_send()
        here = jnp.where(lax.rem(j, 2) == 0, z, last - z)

        @pl.when(here < last)
        def _():
            hop(j, partner).wait_send()

        @pl.when(here > 0)
        def _():
            cast(j, partner).wait_send()

        return carry

    lax.fori_loop(0, count, finish, 0)
    over_out.finish(grad_out)
    over_in.finish(grad_in)


def gradients(fraction, pre, part, velocity, w_out, mixed, rows, cols):
    points, hidden = pre.shape
    features = mixed.shape[1]
    block = features // rows
    count = 32
    dma = pltpu.SemaphoreType.DMA
    vmem = functools.partial(pltpu.VMEM, dtype=jnp.float32)
    anywhere = pl.BlockSpec(memory_space=pl.ANY)
    inside = pl.BlockSpec(memory_space=pltpu.VMEM)
    boxes = 2 if rows == 4 else rows - 1
    copies = max(rows, 6)
    scale = (points * rows) ** -0.5

    def result(*shape):
        return jax.ShapeDtypeStruct(shape, jnp.float32)

    return pl.pallas_call(
        functools.partial(backward_kernel, rows, cols // 2, count, SLACK, scale),
        out_shape=(
            result(block, hidden), result(hidden, block), result(1, hidden), result(1, hidden),
        ),
        in_specs=[inside] * 2 + [anywhere] * 4,
        out_specs=(inside,) * 4,
        scratch_shapes=[
            vmem((points // 2, features)), vmem((points // 2, features)), vmem((points // 2, features)),
            vmem((points, features)), vmem((hidden, features)), vmem((points, features)),
            vmem((hidden, features)), vmem((features, hidden)), vmem((points, hidden)), vmem((1, block)),
            vmem((boxes, hidden, block)), vmem((2, hidden // 2, block)),
            vmem((boxes, block, hidden)), vmem((2, block // 2, hidden)),
            vmem((rows, 2, hidden)),
        ] + [dma((count,))] * 9 + [
            dma((rows,)), dma((1,)), dma((copies,)), dma((copies,)), dma((copies,)), dma((copies,)),
            dma((rows,)), dma((rows,)),
        ],
        compiler_params=params(4),
        name="backward",
    )(fraction[:, None], pre, part, velocity, w_out, mixed)


def body(rows, cols, noise, images, time_index, w_in, time_gain, w_out):
    high = lax.Precision.HIGH
    full_noise, full_images = gathered(noise, images, rows, cols)
    width = full_noise.shape[1]
    noise_count = full_noise.shape[0] * rows
    noise_norms = jnp.sum(full_noise * full_noise, axis=1)
    image_norms = jnp.sum(full_images * full_images, axis=1)
    cross = lax.dot_general(
        full_noise,
        full_images,
        (((1,), (1,)), ((), ())),
        precision=high,
        preferred_element_type=jnp.float32,
    )
    scaled = (noise_norms[:, None] + image_norms[None, :] - 2.0 * cross) / (width * EPSILON)
    weights, row_pot, col_pot = coupled(scaled, rows, cols)
    partial_value = jnp.dot(
        weights, full_images, precision=high, preferred_element_type=jnp.float32
    )
    slice_width = noise.shape[1]
    slice_start = lax.axis_index("col") * slice_width
    whole_targets = total_over_col(partial_value, cols, 2)
    targets = lax.dynamic_slice_in_dim(whole_targets, slice_start, slice_width, 1)
    fraction = (time_index.astype(jnp.float32) + 0.5) / TIMES
    mixed = (1.0 - fraction)[:, None] * full_noise + fraction[:, None] * whole_targets
    velocity = whole_targets - full_noise
    pre = (
        jnp.dot(mixed, w_in, precision=high, preferred_element_type=jnp.float32)
        + fraction[:, None] * time_gain[None, :]
    )
    hidden = pre * jax.nn.sigmoid(pre)
    part_out = jnp.dot(hidden, w_out, precision=high, preferred_element_type=jnp.float32)
    grad_in, grad_out, grad_time, squared_all = gradients(
        fraction, pre, part_out, velocity, w_out, mixed, rows, cols
    )
    mse = squared_all[0, 0] / (noise_count * width)
    return (targets, row_pot, col_pot, grad_in, grad_time[0], grad_out, mse)


def solution(mesh):
    placed = (P("row", "col"), P("col", "row"), P("row"), P(None, "col"), P("col"), P("col", None))
    return jax.shard_map(
        functools.partial(body, mesh.shape["row"], mesh.shape["col"]),
        mesh=mesh,
        in_specs=placed,
        out_specs=(
            P("row", "col"),
            P("row"),
            P("col"),
            P("row", "col"),
            P("col"),
            P("col", "row"),
            P(),
        ),
        check_vma=False,
    )
```
